256 devices in a mesh: seq: 8 (over y_hi, x), tensor: 32 (over y_lo, z, core).
Axes of the slice: x: 4, y: 4 (y_hi: 2, y_lo: 2; y = y_hi * 2 + y_lo), z: 8, core: 2. Of those that a mesh axis runs over, the one named last changes fastest.
Arguments:
- frames: bfloat16 [4096, 8192], P('seq', 'tensor'), may hold values from -6 to 6
- up_factors: bfloat16 [6, 128, 256, 256], P(None, 'tensor'), may hold values from -0.15625 to 0.15625
- down_factors: bfloat16 [6, 128, 256, 256], P(None, 'tensor'), may hold values from -0.078125 to 0.078125
- pattern: int32 [128, 5], P('tensor'), may hold values 0 or 1
- level_bits: int32 [5], replicated, may hold values from 0 to 4, each once
- taps: float32 [3, 8192], P(None, 'tensor'), may hold values from -3 to 3
- cotangent: bfloat16 [4096, 8192], P('seq', 'tensor'), may hold values from -6 to 6
Outputs:
- convolved: bfloat16 [4096, 8192], P('seq', 'tensor')
- grad_frames: bfloat16 [4096, 8192], P('seq', 'tensor')
- grad_up: float32 [6, 128, 256, 256], P(None, 'tensor', 'seq')
- grad_down: float32 [6, 128, 256, 256], P(None, 'tensor', 'seq')
The draws below stay inside these ranges and needn't reach their ends.
Inputs may be any that keep to these rules, and one draw needn't show every extreme that they name: Level l pairs feature block i with block i xor 2^level_bits[l]; each of 0..4 appears once.
All inputs are finite; a program needn't handle non-finite values. No bound on the sum of `pattern` on one device may be relied on, other than what follows from the above.
Results may differ from the reference program's by a relative error of at most 0.012.
Values may be sent and summed in bfloat16 or wider, within the bound.
A program may use at most 64 MiB of HBM per device.

```python
import jax
import jax.numpy as jnp
from jax import lax

D = 8192
H = 32768
BS = 256
LEVELS = 5
FRAMES_DEV = 512
FRAMES = 4096
NHB = 128
N_SEQ = 8


def set_ends(entries, stream_key, least, largest):
    index_at = [jax.random.randint(jax.random.fold_in(stream_key, axis), (), 0, length) for axis, length in enumerate(entries.shape)]
    main_axis = entries.shape.index(max(entries.shape))
    beside = index_at[:main_axis] + [(index_at[main_axis] + 1) % entries.shape[main_axis]] + index_at[main_axis + 1:]
    return entries.at[tuple(index_at)].set(least).at[tuple(beside)].set(largest)


def block_levels(own_key, shape, shards, smallest, largest):
    def one(axis_at, blocks):
        heights = jax.random.uniform(jax.random.fold_in(jax.random.fold_in(own_key, 6), axis_at), (blocks,), jnp.float32, smallest / len(shards), largest / len(shards))
        return jnp.repeat(jnp.exp(heights), shape[axis_at] // blocks).reshape((-1,) + (1,) * (len(shape) - axis_at - 1))

    loudness = one(*shards[0])
    for cut in shards[1:]:
        loudness = loudness * one(*cut)
    return loudness


def scatter_about(stream_key, extent, scale, reach, shards=(), kind=jnp.bfloat16):
    drawn = scale * jax.random.normal(stream_key, extent, jnp.float32)
    if shards:
        drawn = drawn * block_levels(stream_key, extent, shards, -0.22, 0.18)
    return jnp.clip(drawn, -reach, reach).astype(kind)


def setup_inputs(seed: int = 0) -> dict:
    splits = jax.random.split(jax.random.key(seed), 8)
    frames = scatter_about(splits[0], (FRAMES, D), 1.0, 6.0, ((0, 8), (1, 32)))
    up_factors = scatter_about(splits[1], (LEVELS + 1, NHB, BS, BS), ((LEVELS + 1) * BS) ** -0.5, 0.15625, ((1, 32),))
    down_factors = scatter_about(splits[2], (LEVELS + 1, NHB, BS, BS), ((LEVELS + 1) * (H // D) * BS) ** -0.5, 0.078125, ((1, 32),))
    pattern = set_ends((jax.random.randint(splits[3], (NHB, LEVELS), 0, 4) < 3).astype(jnp.int32), jax.random.fold_in(splits[3], 1), 0, 1)
    level_bits = jax.random.permutation(splits[4], LEVELS).astype(jnp.int32)
    taps = scatter_about(splits[5], (3, D), 0.6, 3.0, ((1, 32),), jnp.float32)
    cotangent = scatter_about(splits[6], (FRAMES, D), 1.0, 6.0, ((0, 8), (1, 32)))
    return {"frames": frames, "up_factors": up_factors, "down_factors": down_factors, "pattern": pattern, "level_bits": level_bits, "taps": taps, "cotangent": cotangent}


coef = 0.7978845608028654

def gelu_value(u):
    return 0.5 * u * (1.0 + jnp.tanh(coef * (u + 0.044715 * u * u * u)))

def gelu_slope(u):
    inner = jnp.tanh(coef * (u + 0.044715 * u * u * u))
    return 0.5 * (1.0 + inner) + 0.5 * u * (1.0 - inner * inner) * coef * (1.0 + 3.0 * 0.044715 * u * u)

def reference(frames, up_factors, down_factors, pattern, level_bits, taps, cotangent):
    f32 = jnp.float32
    nblocks = D // BS
    ratio = H // D
    upf = up_factors.reshape(LEVELS + 1, nblocks, ratio, BS, BS)
    downf = down_factors.reshape(LEVELS + 1, nblocks, ratio, BS, BS)
    masks = pattern.reshape(nblocks, ratio, LEVELS).astype(f32)
    blocks = jnp.arange(nblocks, dtype=jnp.int32)
    partners = [jnp.bitwise_xor(blocks, jnp.left_shift(jnp.int32(1), level_bits[lev]).astype(jnp.int32)) for lev in range(LEVELS)]
    inputs = frames.reshape(FRAMES, nblocks, BS).astype(f32)
    pre = jnp.einsum('rbs,bhsf->rbhf', inputs, upf[0].astype(f32))
    for lev in range(LEVELS):
        moved = inputs[:, partners[lev]]
        pre = pre + masks[None, :, :, lev, None] * jnp.einsum('rbs,bhsf->rbhf', moved, upf[lev + 1].astype(f32))
    hidden = gelu_value(pre).astype(jnp.bfloat16)
    hidf = hidden.astype(f32)
    mixed = jnp.einsum('rbhf,bhfs->rbs', hidf, downf[0].astype(f32))
    for lev in range(LEVELS):
        masked = (hidden * masks[None, :, :, lev, None].astype(jnp.bfloat16)).astype(f32)
        part = jnp.einsum('rbhf,bhfs->rbs', masked, downf[lev + 1].astype(f32))
        mixed = mixed + part[:, partners[lev]]
    mixed = mixed.reshape(FRAMES, D).astype(jnp.bfloat16)
    padded = jnp.pad(mixed.astype(f32), ((1, 1), (0, 0)))
    convolved = (taps[0] * padded[:-2] + taps[1] * padded[1:-1] + taps[2] * padded[2:]).astype(jnp.bfloat16)
    gpad = jnp.pad(cotangent.astype(f32), ((1, 1), (0, 0)))
    grad_mixed = (taps[0] * gpad[2:] + taps[1] * gpad[1:-1] + taps[2] * gpad[:-2]).astype(jnp.bfloat16)
    gmix = grad_mixed.reshape(FRAMES, nblocks, BS).astype(f32)
    grad_hidden = jnp.einsum('rbs,bhfs->rbhf', gmix, downf[0].astype(f32))
    for lev in range(LEVELS):
        moved = gmix[:, partners[lev]]
        grad_hidden = grad_hidden + masks[None, :, :, lev, None] * jnp.einsum('rbs,bhfs->rbhf', moved, downf[lev + 1].astype(f32))
    grad_pre = (grad_hidden * gelu_slope(pre)).astype(jnp.bfloat16)
    gpre = grad_pre.astype(f32)
    grad_in = jnp.einsum('rbhf,bhsf->rbs', gpre, upf[0].astype(f32))
    for lev in range(LEVELS):
        masked = (grad_pre * masks[None, :, :, lev, None].astype(jnp.bfloat16)).astype(f32)
        part = jnp.einsum('rbhf,bhsf->rbs', masked, upf[lev + 1].astype(f32))
        grad_in = grad_in + part[:, partners[lev]]
    grad_frames = grad_in.reshape(FRAMES, D).astype(jnp.bfloat16)
    scale = 1.0 / jnp.sqrt(jnp.asarray(FRAMES, f32))

    def group_sum(left, right):
        left_q = left.reshape(N_SEQ, FRAMES_DEV, nblocks, -1)
        right_q = right.reshape(N_SEQ, FRAMES_DEV, nblocks, ratio, BS)
        return (left_q, right_q)

    def reduce_terms(terms):
        rounded = (terms * scale).astype(jnp.bfloat16)
        rounded = lax.optimization_barrier(rounded)
        return lax.optimization_barrier(jnp.sum(rounded.astype(f32), axis=0))
    up_list = []
    down_list = []
    for lev in range(LEVELS + 1):
        if lev == 0:
            inp_l = inputs
            gm_l = gmix
            weight = jnp.ones((nblocks, ratio), f32)
        else:
            inp_l = inputs[:, partners[lev - 1]]
            gm_l = gmix[:, partners[lev - 1]]
            weight = masks[:, :, lev - 1]
        left_q, right_q = group_sum(inp_l, gpre)
        terms = jnp.einsum('qrbs,qrbhf->qbhsf', left_q, right_q) * weight[None, :, :, None, None]
        up_list.append(reduce_terms(terms))
        hid_q = hidf.reshape(N_SEQ, FRAMES_DEV, nblocks, ratio, BS)
        gm_q = gm_l.reshape(N_SEQ, FRAMES_DEV, nblocks, BS)
        terms = jnp.einsum('qrbhf,qrbs->qbhfs', hid_q, gm_q) * weight[None, :, :, None, None]
        down_list.append(reduce_terms(terms))
    grad_up = jnp.stack(up_list).reshape(LEVELS + 1, H // BS, BS, BS)
    grad_down = jnp.stack(down_list).reshape(LEVELS + 1, H // BS, BS, BS)
    return (convolved, grad_frames, grad_up, grad_down)
```

```python
import functools

import jax
import jax.numpy as jnp
from jax import lax
from jax.experimental import pallas as pl
from jax.experimental.pallas import tpu as pltpu
from jax.sharding import PartitionSpec as P

COEF = 0.7978845608028654
F32 = jnp.float32
BF16 = jnp.bfloat16
CHUNKS = 4
N_SEMS = 160


def dot_nn(a, b):
    return jnp.dot(a, b, preferred_element_type=F32)


def dot_nt(a, b):
    return lax.dot_general(a, b, (((1,), (1,)), ((), ())), preferred_element_type=F32)


class Net:
    def __init__(self, ssem, rsem):
        self.ssem, self.rsem, self.count, self.sent = ssem, rsem, 0, []

    def send(self, src, dst, device):
        i = self.count
        self.count += 1
        copy = pltpu.make_async_remote_copy(
            src_ref=src,
            dst_ref=dst,
            send_sem=self.ssem.at[i],
            recv_sem=self.rsem.at[i],
            device_id=device,
            device_id_type=pl.DeviceIdType.MESH,
        )
        copy.start()
        self.sent.append(copy)
        return copy


def kernel(
    bits,
    pattern,
    frames,
    cot,
    taps,
    up_hbm,
    down_hbm,
    conv_out,
    gin_out,
    gup_out,
    gdown_out,
    up_raw,
    down_raw,
    wu,
    wd,
    xs,
    gs,
    xt,
    pre,
    gh,
    hid,
    hidt,
    gpre,
    part,
    part_f,
    relay,
    got,
    term,
    ra,
    rb,
    ea,
    eb,
    from_left,
    from_right,
    ysend,
    yrecv,
    mine,
    halo,
    pad,
    mix,
    wsem,
    ssem,
    rsem,
):
    rows, width = frames.shape
    chunk = rows // CHUNKS
    half = rows // 2
    ratio = wu.shape[1]
    s = lax.axis_index("seq")
    t = lax.axis_index("tensor")
    x, yh = s % 4, s // 4

    def flip(*which):
        out = t
        for b in which:
            out = out + (1 << b) * (1 - 2 * ((t // (1 << b)) % 2))
        return {"tensor": out}

    to_core, to_z1, to_z2, to_z6, to_y = flip(0), flip(1), flip(2), flip(2, 3), flip(4)
    x_right, x_left = {"seq": yh * 4 + (x + 1) % 4}, {"seq": yh * 4 + (x + 3) % 4}
    y_far = {"seq": (1 - yh) * 4 + x}
    s_next, s_prev = {"seq": (s + 1) % 8}, {"seq": (s + 7) % 8}
    net = Net(ssem, rsem)

    copy_up = pltpu.make_async_copy(up_hbm, up_raw, wsem.at[0])
    copy_down = pltpu.make_async_copy(down_hbm, down_raw, wsem.at[1])
    copy_up.start()
    copy_down.start()

    barrier = pltpu.get_barrier_semaphore()
    peers = (to_core, to_z1, to_z2, to_z6, to_y, x_right, x_left, y_far, s_next, s_prev)
    for peer in peers:
        pl.semaphore_signal(barrier, inc=1, device_id=peer, device_id_type=pl.DeviceIdType.MESH)
    pl.semaphore_wait(barrier, len(peers))

    def halo_send(ref, kind):
        return (
            net.send(ref.at[pl.ds(rows - 16, 16)], halo.at[kind, 0], s_next),
            net.send(ref.at[pl.ds(0, 16)], halo.at[kind, 1], s_prev),
        )

    def piece(c):
        return pl.ds(c * chunk, chunk)

    def spread(own, dst):
        z2 = [net.send(own.at[piece(c)], dst.at[3, piece(c)], to_z2) for c in range(CHUNKS)]
        z1 = net.send(own, dst.at[2], to_z1)
        y = net.send(own, dst.at[5], to_y)
        core = net.send(own, dst.at[1], to_core)
        return z2, z1, y, core

    def forward(z2, dst):
        z4 = []
        for c in range(CHUNKS):
            z2[c].wait_recv()
            z4.append(net.send(dst.at[3, piece(c)], dst.at[4, piece(c)], to_z6))
        return z4

    cot_halo = halo_send(cot, 0)
    x_z2, x_z1, x_y, x_core = spread(frames, xs)

    level_of = []
    for b in range(5):
        found = jnp.int32(1)
        for lev in range(1, 5):
            found = jnp.where(bits[lev] == b, lev + 1, found)
        level_of.append(found)
    mask_of = [[jnp.float32(1.0)] * ratio] + [
        [
            sum(jnp.where(bits[lev] == b, pattern[k, lev], 0) for lev in range(5)).astype(F32)
            for k in range(ratio)
        ]
        for b in range(5)
    ]

    def build(raw, out):
        for k in range(ratio):
            out[0, k] = raw[0, k]
        for b in range(5):
            for k in range(ratio):
                out[b + 1, k] = (raw[level_of[b], k].astype(F32) * mask_of[b + 1][k]).astype(BF16)

    def accumulate(acc, lhs, weights, b, dot, first=False):
        def body(k, carry):
            value = dot(lhs[...], weights[b, k])
            if first:
                acc[k] = value
            else:
                acc[k] += value
            return carry

        lax.fori_loop(0, ratio, body, 0)

    def convolve(ref, kind, before, after):
        prev = halo[kind, 0].astype(F32)[15:16]
        nxt = halo[kind, 1].astype(F32)[0:1]
        pad[pl.ds(7, 1)] = jnp.where(s > 0, prev, 0.0)
        pad[pl.ds(8, rows)] = ref[...].astype(F32)
        pad[pl.ds(8 + rows, 1)] = jnp.where(s < 7, nxt, 0.0)
        return (
            before * pad[pl.ds(7, rows)] + taps[1:2] * pad[pl.ds(8, rows)] + after * pad[pl.ds(9, rows)]
        ).astype(BF16)

    copy_up.wait()
    build(up_raw, wu)
    accumulate(pre, frames, wu, 0, dot_nn, first=True)
    for copy in cot_halo:
        copy.wait_recv()
    gs[0] = convolve(cot, 0, taps[2:3], taps[0:1])
    x_z4 = forward(x_z2, xs)
    g_z2, g_z1, g_y, g_core = spread(gs.at[0], gs)
    copy_down.wait()
    build(down_raw, wd)
    x_core.wait_recv()
    accumulate(pre, xs.at[1], wu, 1, dot_nn)
    x_y.wait_recv()
    accumulate(pre, xs.at[5], wu, 5, dot_nn)
    accumulate(pre, xs.at[3], wu, 3, dot_nn)
    x_z1.wait_recv()
    accumulate(pre, xs.at[2], wu, 2, dot_nn)
    xt[0] = frames[...].T
    for b in (1, 5, 3, 2):
        xt[b] = xs[b].T

    def partial_rows(source, weights, b, dot, at):
        total = dot(source[0, at], weights[b, 0])
        for k in range(1, ratio):
            total += dot(source[k, at], weights[b, k])
        return total

    whole = pl.ds(0, rows)

    mixed_z4 = []
    for h in range(2):
        for c in (2 * h, 2 * h + 1):
            x_z4[c].wait_recv()
        at = pl.ds(h * half, half)

        def finish(k, carry, at=at):
            u = pre[k, at] + dot_nn(xs[4, at], wu[4, k])
            square = u * u
            inner = jnp.tanh(COEF * (u + 0.044715 * square * u))
            hid[k, at] = (0.5 * u * (1.0 + inner)).astype(BF16)
            pre[k, at] = 0.5 * (1.0 + inner) + 0.5 * u * (1.0 - inner * inner) * COEF * (
                1.0 + 3.0 * 0.044715 * square
            )
            return carry

        lax.fori_loop(0, ratio, finish, 0)
        part[0, 0, at] = partial_rows(hid, wd, 4, dot_nn, at).astype(BF16)
        for c in (2 * h, 2 * h + 1):
            mixed_z4.append(net.send(part.at[0, 0, piece(c)], got.at[0, 4, piece(c)], to_z6))
    g_z4 = forward(g_z2, gs)

    def partials(phase, source, weights, dot):
        sends = []
        for slot, b, device in ((1, 2, to_z1), (2, 5, to_y), (3, 1, to_core)):
            part[phase, slot] = partial_rows(source, weights, b, dot, whole).astype(BF16)
            sends.append(net.send(part.at[phase, slot], got.at[phase, slot], device))
        part_f[phase, 0] = partial_rows(source, weights, 3, dot, whole)
        part_f[phase, 1] = partial_rows(source, weights, 0, dot, whole)
        return sends

    def combine(phase, z4):
        sends = []
        for c in range(CHUNKS):
            z4[c].wait_recv()
            at = piece(c)
            relay[phase, at] = (part_f[phase, 0, at] + got[phase, 4, at].astype(F32)).astype(BF16)
            sends.append(net.send(relay.at[phase, at], got.at[phase, 0, at], to_z2))
        return sends

    def gather_sum(phase, waits):
        for copy in waits:
            copy.wait_recv()
        total = part_f[phase, 1]
        for slot in range(4):
            total += got[phase, slot].astype(F32)
        return total.astype(BF16)

    mixed_sends = partials(0, hid, wd, dot_nn)

    for k in range(ratio):
        hidt[k] = hid[k].T

    scale = 1.0 / 64.0
    flows = {}

    def scatter_one(g):
        far, right, left = (x + 2) % 4, (x + 1) % 4, (x + 3) % 4
        flows[g] = (
            net.send(term.at[g, far], ra.at[g], x_right),
            net.send(term.at[g, 4 + far], rb.at[g], x_left),
            net.send(term.at[g, 4 + right], from_left.at[g, 1], x_right),
            net.send(term.at[g, left], from_right.at[g, 0], x_left),
        )

    def scatter_two(g):
        via_right, via_left, own_b, own_a = flows[g]
        right, left = (x + 1) % 4, (x + 3) % 4
        via_right.wait_recv()
        ea[g] = (ra[g].astype(F32) + term[g, right].astype(F32)).astype(BF16)
        sum_a = net.send(ea.at[g], from_left.at[g, 0], x_right)
        via_left.wait_recv()
        eb[g] = (rb[g].astype(F32) + term[g, 4 + left].astype(F32)).astype(BF16)
        sum_b = net.send(eb.at[g], from_right.at[g, 1], x_left)
        flows[g] = (own_b, own_a, sum_a, sum_b)

    def side_sum(g, h):
        return (
            term[g, h * 4 + x].astype(F32) + from_left[g, h].astype(F32) + from_right[g, h].astype(F32)
        )

    def scatter_three(g):
        for copy in flows[g]:
            copy.wait_recv()
        ysend[g] = side_sum(g, 1 - yh).astype(BF16)
        flows[g] = net.send(ysend.at[g], yrecv.at[g], y_far)
        mine[g] = side_sum(g, yh)

    def down_term(b):
        for k in range(ratio):
            value = dot_nn(hidt[k], gs[b]) * (mask_of[b][k] * scale)
            term[b, :, k] = value.astype(BF16).reshape(8, 32, width)
        scatter_one(b)

    def up_term(b):
        for k in range(ratio):
            value = dot_nn(xt[b], gpre[k]) * (mask_of[b][k] * scale)
            term[6 + b, :, k] = value.astype(BF16).reshape(8, 32, width)
        scatter_one(6 + b)

    down_term(0)
    accumulate(gh, gs.at[0], wd, 0, dot_nt, first=True)
    g_core.wait_recv()
    down_term(1)
    accumulate(gh, gs.at[1], wd, 1, dot_nt)
    g_y.wait_recv()
    down_term(5)
    accumulate(gh, gs.at[5], wd, 5, dot_nt)
    mixed_z2 = combine(0, mixed_z4)
    accumulate(gh, gs.at[3], wd, 3, dot_nt)
    down_term(3)
    scatter_two(0)
    g_z1.wait_recv()
    accumulate(gh, gs.at[2], wd, 2, dot_nt)
    down_term(2)
    scatter_two(1)
    xt[4] = xs[4].T

    gin_z4 = []
    for h in range(2):
        for c in (2 * h, 2 * h + 1):
            g_z4[c].wait_recv()
        at = pl.ds(h * half, half)

        def finish_grad(k, carry, at=at):
            gpre[k, at] = ((gh[k, at] + dot_nt(gs[4, at], wd[4, k])) * pre[k, at]).astype(BF16)
            return carry

        lax.fori_loop(0, ratio, finish_grad, 0)
        part[1, 0, at] = partial_rows(gpre, wu, 4, dot_nt, at).astype(BF16)
        for c in (2 * h, 2 * h + 1):
            gin_z4.append(net.send(part.at[1, 0, piece(c)], got.at[1, 4, piece(c)], to_z6))
    up_term(0)
    gin_sends = partials(1, gpre, wu, dot_nt)
    down_term(4)
    up_term(1)
    scatter_two(5)
    up_term(5)
    gin_z2 = combine(1, gin_z4)
    scatter_two(3)
    up_term(2)
    scatter_two(2)
    up_term(3)
    scatter_two(6)
    up_term(4)
    scatter_three(0)
    scatter_three(1)
    mix[...] = gather_sum(0, mixed_z2 + mixed_sends)
    mix_halo = halo_send(mix, 1)
    scatter_two(4)
    scatter_three(5)
    scatter_two(7)
    scatter_three(3)
    scatter_two(11)
    scatter_three(2)
    for copy in mix_halo:
        copy.wait_recv()
    conv_out[...] = convolve(mix, 1, taps[0:1], taps[2:3])
    scatter_two(8)
    scatter_three(6)
    scatter_three(4)
    scatter_two(9)
    scatter_three(7)
    scatter_two(10)
    scatter_three(11)
    gin_out[...] = gather_sum(1, gin_z2 + gin_sends)
    for g in (8, 9, 10):
        scatter_three(g)
    for g in range(12):
        flows[g].wait_recv()
    for base, out in ((6, gup_out), (0, gdown_out)):
        out[0] = mine[base] + yrecv[base].astype(F32)
        for lev in range(5):
            g = base + 1 + bits[lev]
            out[lev + 1] = mine[g] + yrecv[g].astype(F32)
    for copy in net.sent:
        copy.wait_send()


def local(frames, up_factors, down_factors, pattern, level_bits, taps, cotangent):
    rows, width = frames.shape
    factors, ratio, _, _ = up_factors.shape
    weights = (factors, ratio, width, width)
    tile = (ratio, 32, width)
    vmem = pl.BlockSpec(memory_space=pltpu.VMEM)
    smem = pl.BlockSpec(memory_space=pltpu.SMEM)
    anywhere = pl.BlockSpec(memory_space=pl.ANY)
    shape = jax.ShapeDtypeStruct
    return pl.pallas_call(
        kernel,
        out_shape=(
            shape((rows, width), BF16),
            shape((rows, width), BF16),
            shape((factors,) + tile, F32),
            shape((factors,) + tile, F32),
        ),
        in_specs=[smem, smem, vmem, vmem, vmem, anywhere, anywhere],
        out_specs=(vmem,) * 4,
        scratch_shapes=[
            pltpu.VMEM(weights, BF16),
            pltpu.VMEM(weights, BF16),
            pltpu.VMEM(weights, BF16),
            pltpu.VMEM(weights, BF16),
            pltpu.VMEM((6, rows, width), BF16),
            pltpu.VMEM((6, rows, width), BF16),
            pltpu.VMEM((6, width, rows), BF16),
            pltpu.VMEM((ratio, rows, width), F32),
            pltpu.VMEM((ratio, rows, width), F32),
            pltpu.VMEM((ratio, rows, width), BF16),
            pltpu.VMEM((ratio, width, rows), BF16),
            pltpu.VMEM((ratio, rows, width), BF16),
            pltpu.VMEM((2, 4, rows, width), BF16),
            pltpu.VMEM((2, 2, rows, width), F32),
            pltpu.VMEM((2, rows, width), BF16),
            pltpu.VMEM((2, 5, rows, width), BF16),
            pltpu.VMEM((12, 8) + tile, BF16),
            pltpu.VMEM((12,) + tile, BF16),
            pltpu.VMEM((12,) + tile, BF16),
            pltpu.VMEM((12,) + tile, BF16),
            pltpu.VMEM((12,) + tile, BF16),
            pltpu.VMEM((12, 2) + tile, BF16),
            pltpu.VMEM((12, 2) + tile, BF16),
            pltpu.VMEM((12,) + tile, BF16),
            pltpu.VMEM((12,) + tile, BF16),
            pltpu.VMEM((12,) + tile, F32),
            pltpu.VMEM((2, 2, 16, width), BF16),
            pltpu.VMEM((rows + 16, width), F32),
            pltpu.VMEM((rows, width), BF16),
            pltpu.SemaphoreType.DMA((2,)),
            pltpu.SemaphoreType.DMA((N_SEMS,)),
            pltpu.SemaphoreType.DMA((N_SEMS,)),
        ],
        compiler_params=pltpu.CompilerParams(
            collective_id=0, has_side_effects=True, vmem_limit_bytes=62 * 1024 * 1024
        ),
    )(level_bits, pattern, frames, cotangent, taps, up_factors, down_factors)


def solution(mesh):
    in_specs = (
        P("seq", "tensor"),
        P(None, "tensor", None, None),
        P(None, "tensor", None, None),
        P("tensor", None),
        P(),
        P(None, "tensor"),
        P("seq", "tensor"),
    )
    out_specs = (
        P("seq", "tensor"),
        P("seq", "tensor"),
        P(None, "tensor", "seq", None),
        P(None, "tensor", "seq", None),
    )
    return jax.shard_map(local, mesh=mesh, in_specs=in_specs, out_specs=out_specs, check_vma=False)
```

```python
import functools

import jax
import jax.numpy as jnp
from jax import lax
from jax.experimental import pallas as pl
from jax.experimental.pallas import tpu as pltpu
from jax.sharding import PartitionSpec as P

COEF = 0.7978845608028654
F32 = jnp.float32
BF16 = jnp.bfloat16
CHUNKS = 4
N_SENDS = 18
N_RECVS = 66
Y_FIRST = (3, 7, 11)


def dot_nn(a, b):
    return jnp.dot(a, b, preferred_element_type=F32)


def dot_nt(a, b):
    return lax.dot_general(a, b, (((1,), (1,)), ((), ())), preferred_element_type=F32)


class Net:
    def __init__(self, ssem, rsem):
        self.ssem, self.rsem, self.n_send, self.n_recv, self.ends = ssem, rsem, 0, 0, []

    def sender(self, size):
        sem = self.ssem.at[self.n_send]
        self.n_send += 1
        self.ends.append((size, sem))
        return sem

    def receiver(self):
        sem = self.rsem.at[self.n_recv]
        self.n_recv += 1
        return sem

    def send(self, src, dst, device, ssem, rsem=None):
        rsem = self.receiver() if rsem is None else rsem
        pltpu.make_async_remote_copy(
            src_ref=src,
            dst_ref=dst,
            send_sem=ssem,
            recv_sem=rsem,
            device_id=device,
            device_id_type=pl.DeviceIdType.MESH,
        ).start()
        return dst, rsem

    def finish(self):
        for size, sem in self.ends:
            arrive((size, sem))


def arrive(flow):
    ref, sem = flow
    pltpu.make_async_copy(ref, ref, sem).wait()


def kernel(
    bits,
    pattern,
    frames_in,
    cot_in,
    taps,
    up_hbm,
    down_hbm,
    conv_hbm,
    gin_hbm,
    gup_hbm,
    gdown_hbm,
    cot,
    conv_out,
    gin_out,
    gup_out,
    gdown_out,
    up_raw,
    down_raw,
    wu,
    wd,
    xs,
    gs,
    xt,
    pre,
    gh,
    hid,
    hidt,
    gpre,
    part,
    part_f,
    relay,
    got,
    term,
    rab,
    eab,
    side,
    ybig,
    comb,
    ysend,
    yrecv_down,
    yrecv_up,
    mine,
    halo,
    pad,
    mix,
    wsem,
    ssem,
    rsem,
):
    rows, width = frames_in.shape
    frames = xs.at[0]
    yrecv = (yrecv_down, yrecv_up)
    chunk = rows // CHUNKS
    half = rows // 2
    ratio = wu.shape[1]
    s = lax.axis_index("seq")
    t = lax.axis_index("tensor")
    x, yh = s % 4, s // 4

    def flip(*which):
        out = t
        for b in which:
            out = out + (1 << b) * (1 - 2 * ((t // (1 << b)) % 2))
        return {"tensor": out}

    to_core, to_z1, to_z2, to_z6, to_y = flip(0), flip(1), flip(2), flip(2, 3), flip(4)
    x_right, x_left = {"seq": yh * 4 + (x + 1) % 4}, {"seq": yh * 4 + (x + 3) % 4}
    y_far = {"seq": (1 - yh) * 4 + x}
    s_next, s_prev = {"seq": (s + 1) % 8}, {"seq": (s + 7) % 8}
    net = Net(ssem, rsem)

    barrier = pltpu.get_barrier_semaphore()
    peers = (to_core, to_z1, to_z2, to_z6, to_y, x_right, x_left, y_far, s_next, s_prev)
    for peer in peers:
        pl.semaphore_signal(barrier, inc=1, device_id=peer, device_id_type=pl.DeviceIdType.MESH)

    def fetch(src, dst, i):
        copy = pltpu.make_async_copy(src, dst, wsem.at[i])
        copy.start()
        return copy

    copy_frames = fetch(frames_in, frames, 2)
    copy_up = fetch(up_hbm, up_raw, 0)
    copy_cot = fetch(cot_in, cot, 3)
    copy_down = fetch(down_hbm, down_raw, 1)
    pl.semaphore_wait(barrier, len(peers))

    def halo_send(ref, kind):
        out, into = net.sender(halo.at[kind]), net.receiver()
        net.send(ref.at[pl.ds(rows - 16, 16)], halo.at[kind, 0], s_next, out, into)
        net.send(ref.at[pl.ds(0, 16)], halo.at[kind, 1], s_prev, out, into)
        return halo.at[kind], into

    def piece(c):
        return pl.ds(c * chunk, chunk)

    def spread(own, dst):
        out = net.sender(dst.at[pl.ds(1, 5)])
        z2 = [net.send(own.at[piece(c)], dst.at[3, piece(c)], to_z2, out) for c in range(CHUNKS)]
        z1 = net.send(own, dst.at[2], to_z1, out)
        y = net.send(own, dst.at[5], to_y, out)
        core = net.send(own, dst.at[1], to_core, out)
        z4 = [(dst.at[4, pl.ds(h * half, half)], net.receiver()) for h in range(2)]
        return out, z2, z1, y, core, z4

    def forward(out, z2, z4, dst, c):
        arrive(z2[c])
        net.send(dst.at[3, piece(c)], dst.at[4, piece(c)], to_z6, out, z4[c // 2][1])

    cot_halo = halo_send(cot_in, 0)
    x_out, x_z2, x_z1, x_y, x_core, x_z4 = spread(frames_in, xs)

    level_of = []
    for b in range(5):
        found = jnp.int32(1)
        for lev in range(1, 5):
            found = jnp.where(bits[lev] == b, lev + 1, found)
        level_of.append(found)
    mask_of = [[jnp.float32(1.0)] * ratio] + [
        [
            sum(jnp.where(bits[lev] == b, pattern[k, lev], 0) for lev in range(5)).astype(F32)
            for k in range(ratio)
        ]
        for b in range(5)
    ]

    def build(raw, out):
        for k in range(ratio):
            out[0, k] = raw[0, k]
        for b in range(5):
            for k in range(ratio):
                out[b + 1, k] = (raw[level_of[b], k].astype(F32) * mask_of[b + 1][k]).astype(BF16)

    def accumulate(acc, lhs, weights, b, dot, first=False):
        def body(k, carry):
            value = dot(lhs[...], weights[b, k])
            if first:
                acc[k] = value
            else:
                acc[k] += value
            return carry

        lax.fori_loop(0, ratio, body, 0)

    def convolve(ref, kind, before, after):
        prev = halo[kind, 0].astype(F32)[15:16]
        nxt = halo[kind, 1].astype(F32)[0:1]
        pad[pl.ds(7, 1)] = jnp.where(s > 0, prev, 0.0)
        pad[pl.ds(8, rows)] = ref[...].astype(F32)
        pad[pl.ds(8 + rows, 1)] = jnp.where(s < 7, nxt, 0.0)
        return (
            before * pad[pl.ds(7, rows)] + taps[1:2] * pad[pl.ds(8, rows)] + after * pad[pl.ds(9, rows)]
        ).astype(BF16)

    copy_up.wait()
    build(up_raw, wu)
    copy_frames.wait()
    accumulate(pre, frames, wu, 0, dot_nn, first=True)
    forward(x_out, x_z2, x_z4, xs, 0)
    arrive(x_core)
    accumulate(pre, xs.at[1], wu, 1, dot_nn)
    forward(x_out, x_z2, x_z4, xs, 1)
    copy_down.wait()
    build(down_raw, wd)
    xt[0] = xs[0].T
    xt[1] = xs[1].T
    forward(x_out, x_z2, x_z4, xs, 2)
    arrive(x_y)
    accumulate(pre, xs.at[5], wu, 5, dot_nn)
    forward(x_out, x_z2, x_z4, xs, 3)
    copy_cot.wait()
    arrive(cot_halo)
    gs[0] = convolve(cot, 0, taps[2:3], taps[0:1])
    accumulate(pre, xs.at[3], wu, 3, dot_nn)
    arrive(x_z1)
    accumulate(pre, xs.at[2], wu, 2, dot_nn)
    for b in (5, 3, 2):
        xt[b] = xs[b].T
    for g in Y_FIRST:
        yrecv[g // 6][g % 6] = jnp.zeros(yrecv_up.shape[1:], BF16)

    def partial_rows(source, weights, b, dot, at):
        total = dot(source[0, at], weights[b, 0])
        for k in range(1, ratio):
            total += dot(source[k, at], weights[b, k])
        return total

    whole = pl.ds(0, rows)

    for h in range(2):
        arrive(x_z4[h])
        if h == 0:
            g_out, g_z2, g_z1, g_y, g_core, g_z4 = spread(gs.at[0], gs)
        at = pl.ds(h * half, half)

        def finish(k, carry, at=at):
            u = pre[k, at] + dot_nn(xs[4, at], wu[4, k])
            square = u * u
            inner = jnp.tanh(COEF * (u + 0.044715 * square * u))
            hid[k, at] = (0.5 * u * (1.0 + inner)).astype(BF16)
            pre[k, at] = 0.5 * (1.0 + inner) + 0.5 * u * (1.0 - inner * inner) * COEF * (
                1.0 + 3.0 * 0.044715 * square
            )
            return carry

        lax.fori_loop(0, ratio, finish, 0)
    for k in range(ratio):
        hidt[k] = hid[k].T

    phase_out = [net.sender(xs.at[pl.ds(1, 5)]) for _ in range(2)]
    phase_in = [(got.at[p, pl.ds(0, 4)], net.receiver()) for p in range(2)]

    def far_partial(phase, source, weights, dot):
        part[phase, 0] = partial_rows(source, weights, 4, dot, whole).astype(BF16)

    def far_send(phase):
        return [
            net.send(part.at[phase, 0, piece(c)], got.at[phase, 4, piece(c)], to_z6, phase_out[phase])
            for c in range(CHUNKS)
        ]

    def near_send(phase, slot, device):
        net.send(part.at[phase, slot], got.at[phase, slot], device, phase_out[phase], phase_in[phase][1])

    def near_partials(phase, source, weights, dot):
        for slot, b, device in ((2, 5, to_y), (3, 1, to_core), (1, 2, None)):
            part[phase, slot] = partial_rows(source, weights, b, dot, whole).astype(BF16)
            if device is not None:
                near_send(phase, slot, device)

    def kept_partials(phase, source, weights, dot):
        part_f[phase, 0] = partial_rows(source, weights, 3, dot, whole)
        part_f[phase, 1] = partial_rows(source, weights, 0, dot, whole)

    def combine(phase, z4):
        for c in range(CHUNKS):
            arrive(z4[c])
            at = piece(c)
            relay[phase, at] = (part_f[phase, 0, at] + got[phase, 4, at].astype(F32)).astype(BF16)
            net.send(
                relay.at[phase, at], got.at[phase, 0, at], to_z2, phase_out[phase], phase_in[phase][1]
            )

    def gather_sum(phase):
        arrive(phase_in[phase])
        total = part_f[phase, 1]
        for slot in range(4):
            total += got[phase, slot].astype(F32)
        return total.astype(BF16)

    scale = 1.0 / 64.0
    far, right, left = (x + 2) % 4, (x + 1) % 4, (x + 3) % 4
    group_out = {}
    flows = {}

    def halves(g):
        if g in Y_FIRST:
            i = Y_FIRST.index(g)
            first, second = pl.ds(0, ratio // 2), pl.ds(ratio // 2, ratio // 2)
            return comb, (lambda j: (i, j, first)), (lambda j: (i, j, second)), first
        return term, (lambda j: (g, j)), (lambda j: (g, 4 + j)), pl.ds(0, ratio)

    def send_across(g):
        group_out[g] = net.sender(term.at[g, pl.ds(0, 7)])
        i = Y_FIRST.index(g)
        flows[g] = net.send(term.at[g, pl.ds((1 - yh) * 4, 4)], ybig.at[i], y_far, group_out[g])

    def scatter_one(g):
        if g in Y_FIRST:
            i = Y_FIRST.index(g)
            arrive(flows[g])
            comb[i] = (term[g, pl.ds(yh * 4, 4)].astype(F32) + ybig[i].astype(F32)).astype(BF16)
        else:
            group_out[g] = net.sender(term.at[g, pl.ds(0, 7)])
        ref, a_at, b_at, ks = halves(g)
        out, via, end = group_out[g], net.receiver(), net.receiver()
        net.send(ref.at[a_at(far)], rab.at[g, 0, ks], x_right, out, via)
        net.send(ref.at[b_at(far)], rab.at[g, 1, ks], x_left, out, via)
        net.send(ref.at[b_at(right)], side.at[g, 0, 1, ks], x_right, out, end)
        net.send(ref.at[a_at(left)], side.at[g, 1, 0, ks], x_left, out, end)
        flows[g] = ((rab.at[g, :, ks], via), (side.at[g, :, :, ks], end))

    def scatter_two(g):
        ref, a_at, b_at, ks = halves(g)
        arrive(flows[g][0])
        end = flows[g][1][1]
        eab[g, 0, ks] = (rab[g, 0, ks].astype(F32) + ref[a_at(right)].astype(F32)).astype(BF16)
        net.send(eab.at[g, 0, ks], side.at[g, 0, 0, ks], x_right, group_out[g], end)
        eab[g, 1, ks] = (rab[g, 1, ks].astype(F32) + ref[b_at(left)].astype(F32)).astype(BF16)
        net.send(eab.at[g, 1, ks], side.at[g, 1, 1, ks], x_left, group_out[g], end)

    def side_sum(g, own, h, ks):
        return own.astype(F32) + side[g, 0, h, ks].astype(F32) + side[g, 1, h, ks].astype(F32)

    def scatter_three(g):
        arrive(flows[g][1])
        ref, a_at, b_at, ks = halves(g)
        if g in Y_FIRST:
            mine[g, ks] = side_sum(g, ref[a_at(x)], 0, ks)
            mine[g, pl.ds(ratio // 2, ratio // 2)] = side_sum(g, ref[b_at(x)], 1, ks)
            return
        ysend[g] = side_sum(g, term[g, (1 - yh) * 4 + x], 1 - yh, ks).astype(BF16)
        flows[g] = net.send(ysend.at[g], yrecv[g // 6].at[g % 6], y_far, group_out[g])
        mine[g] = side_sum(g, term[g, yh * 4 + x], yh, ks)

    def start(g):
        if g in Y_FIRST:
            send_across(g)
        else:
            scatter_one(g)

    def down_term(b):
        for k in range(ratio):
            value = dot_nn(hidt[k], gs[b]) * (mask_of[b][k] * scale)
            term[b, :, k] = value.astype(BF16).reshape(8, 32, width)
        start(b)

    def up_term(b):
        for k in range(ratio):
            value = dot_nn(xt[b], gpre[k]) * (mask_of[b][k] * scale)
            term[6 + b, :, k] = value.astype(BF16).reshape(8, 32, width)
        start(6 + b)

    down_term(0)
    arrive(g_core)
    down_term(1)
    accumulate(gh, gs.at[0], wd, 0, dot_nt, first=True)
    accumulate(gh, gs.at[1], wd, 1, dot_nt)
    far_partial(0, hid, wd, dot_nn)
    forward(g_out, g_z2, g_z4, gs, 0)
    arrive(g_y)
    down_term(5)
    accumulate(gh, gs.at[5], wd, 5, dot_nt)
    forward(g_out, g_z2, g_z4, gs, 1)
    scatter_two(0)
    kept_partials(0, hid, wd, dot_nn)
    forward(g_out, g_z2, g_z4, gs, 2)
    scatter_two(1)
    forward(g_out, g_z2, g_z4, gs, 3)
    down_term(3)
    near_partials(0, hid, wd, dot_nn)
    accumulate(gh, gs.at[3], wd, 3, dot_nt)
    arrive(g_z1)
    down_term(2)
    accumulate(gh, gs.at[2], wd, 2, dot_nt)
    scatter_two(5)
    xt[4] = xs[4].T
    for h in range(2):
        arrive(g_z4[h])
        at = pl.ds(h * half, half)

        def finish_grad(k, carry, at=at):
            gpre[k, at] = ((gh[k, at] + dot_nt(gs[4, at], wd[4, k])) * pre[k, at]).astype(BF16)
            return carry

        lax.fori_loop(0, ratio, finish_grad, 0)
        if h == 0:
            scatter_one(3)
    mixed_z4 = far_send(0)
    up_term(0)
    far_partial(1, gpre, wu, dot_nt)
    gin_z4 = far_send(1)
    near_send(0, 1, to_z1)
    down_term(4)
    scatter_two(2)
    up_term(1)
    up_term(2)
    up_term(5)
    scatter_two(3)
    up_term(4)
    up_term(3)
    near_partials(1, gpre, wu, dot_nt)
    kept_partials(1, gpre, wu, dot_nt)
    for g in (0, 1, 5):
        scatter_three(g)
    scatter_two(6)
    scatter_two(4)
    combine(0, mixed_z4)
    scatter_two(8)
    scatter_one(7)
    scatter_two(10)
    combine(1, gin_z4)
    near_send(1, 1, to_z1)
    for g in (2, 3):
        scatter_three(g)
    scatter_one(11)
    scatter_two(9)
    scatter_three(6)
    scatter_three(4)
    scatter_two(7)
    mix[...] = gather_sum(0)
    mix_halo = halo_send(mix, 1)
    scatter_two(11)
    scatter_three(8)
    scatter_three(10)
    scatter_three(9)

    def final(base, out):
        there = yrecv[base // 6]
        out[0] = mine[base] + there[0].astype(F32)
        for lev in range(5):
            b = 1 + bits[lev]
            out[lev + 1] = mine[base + b] + there[b].astype(F32)

    for g in (0, 1, 5, 2, 4):
        arrive(flows[g])
    final(0, gdown_out)
    put_gdown = fetch(gdown_out, gdown_hbm, 4)
    arrive(mix_halo)
    conv_out[...] = convolve(mix, 1, taps[0:1], taps[2:3])
    put_conv = fetch(conv_out, conv_hbm, 5)
    scatter_three(7)
    scatter_three(11)
    gin_out[...] = gather_sum(1)
    put_gin = fetch(gin_out, gin_hbm, 6)
    for g in (6, 8, 10, 9):
        arrive(flows[g])
    final(6, gup_out)
    put_gup = fetch(gup_out, gup_hbm, 7)
    net.finish()
    for copy in (put_gdown, put_conv, put_gin, put_gup):
        copy.wait()


def write_kernel(*refs):
    ins, outs, held, sems = refs[:4], refs[4:8], refs[8:12], refs[12]
    loads = [pltpu.make_async_copy(ins[i], held[i], sems.at[i]) for i in range(4)]
    stores = [pltpu.make_async_copy(held[i], outs[i], sems.at[4 + i]) for i in range(4)]
    for load in loads:
        load.start()
    for load, store in zip(loads, stores):
        load.wait()
        store.start()
    for store in stores:
        store.wait()


def local(frames, up_factors, down_factors, pattern, level_bits, taps, cotangent):
    rows, width = frames.shape
    factors, ratio, _, _ = up_factors.shape
    weights = (factors, ratio, width, width)
    tile = (ratio, 32, width)
    vmem = pl.BlockSpec(memory_space=pltpu.VMEM)
    smem = pl.BlockSpec(memory_space=pltpu.SMEM)
    anywhere = pl.BlockSpec(memory_space=pl.ANY)
    shape = jax.ShapeDtypeStruct
    results = (
        shape((rows, width), BF16),
        shape((rows, width), BF16),
        shape((factors,) + tile, F32),
        shape((factors,) + tile, F32),
    )
    held = [pltpu.VMEM(each.shape, each.dtype) for each in results]
    computed = pl.pallas_call(
        kernel,
        out_shape=results,
        in_specs=[smem, smem, anywhere, anywhere, vmem, anywhere, anywhere],
        out_specs=(anywhere,) * 4,
        scratch_shapes=[
            pltpu.VMEM((rows, width), BF16),
            *held,
            pltpu.VMEM(weights, BF16),
            pltpu.VMEM(weights, BF16),
            pltpu.VMEM(weights, BF16),
            pltpu.VMEM(weights, BF16),
            pltpu.VMEM((6, rows, width), BF16),
            pltpu.VMEM((6, rows, width), BF16),
            pltpu.VMEM((6, width, rows), BF16),
            pltpu.VMEM((ratio, rows, width), F32),
            pltpu.VMEM((ratio, rows, width), F32),
            pltpu.VMEM((ratio, rows, width), BF16),
            pltpu.VMEM((ratio, width, rows), BF16),
            pltpu.VMEM((ratio, rows, width), BF16),
            pltpu.VMEM((2, 4, rows, width), BF16),
            pltpu.VMEM((2, 2, rows, width), F32),
            pltpu.VMEM((2, rows, width), BF16),
            pltpu.VMEM((2, 5, rows, width), BF16),
            pltpu.VMEM((12, 8) + tile, BF16),
            pltpu.VMEM((12, 2) + tile, BF16),
            pltpu.VMEM((12, 2) + tile, BF16),
            pltpu.VMEM((12, 2, 2) + tile, BF16),
            pltpu.VMEM((len(Y_FIRST), 4) + tile, BF16),
            pltpu.VMEM((len(Y_FIRST), 4) + tile, BF16),
            pltpu.VMEM((12,) + tile, BF16),
            pltpu.VMEM((6,) + tile, BF16),
            pltpu.VMEM((6,) + tile, BF16),
            pltpu.VMEM((12,) + tile, F32),
            pltpu.VMEM((2, 2, 16, width), BF16),
            pltpu.VMEM((rows + 16, width), F32),
            pltpu.VMEM((rows, width), BF16),
            pltpu.SemaphoreType.DMA((8,)),
            pltpu.SemaphoreType.DMA((N_SENDS,)),
            pltpu.SemaphoreType.DMA((N_RECVS,)),
        ],
        compiler_params=pltpu.CompilerParams(
            collective_id=0, has_side_effects=True, vmem_limit_bytes=62 * 1024 * 1024
        ),
    )(level_bits, pattern, frames, cotangent, taps, up_factors, down_factors)
    return pl.pallas_call(
        write_kernel,
        out_shape=results,
        in_specs=[anywhere] * 4,
        out_specs=(anywhere,) * 4,
        scratch_shapes=[*held, pltpu.SemaphoreType.DMA((8,))],
    )(*computed)


def solution(mesh):
    in_specs = (
        P("seq", "tensor"),
        P(None, "tensor", None, None),
        P(None, "tensor", None, None),
        P("tensor", None),
        P(),
        P(None, "tensor"),
        P("seq", "tensor"),
    )
    out_specs = (
        P("seq", "tensor"),
        P("seq", "tensor"),
        P(None, "tensor", "seq", None),
        P(None, "tensor", "seq", None),
    )
    return jax.shard_map(local, mesh=mesh, in_specs=in_specs, out_specs=out_specs, check_vma=False)
```

```python
import functools

import jax
import jax.numpy as jnp
from jax import lax
from jax.experimental import pallas as pl
from jax.experimental.pallas import tpu as pltpu
from jax.sharding import PartitionSpec as P

COEF = 0.7978845608028654
F32 = jnp.float32
BF16 = jnp.bfloat16
CHUNKS = 4
PIECES = 16
N_SENDS = 18
N_RECVS = 90
Y_FIRST = (3, 7, 11)


def dot_nn(a, b):
    return jnp.dot(a, b, preferred_element_type=F32)


def dot_nt(a, b):
    return lax.dot_general(a, b, (((1,), (1,)), ((), ())), preferred_element_type=F32)


class Net:
    def __init__(self, ssem, rsem):
        self.ssem, self.rsem, self.n_send, self.n_recv, self.ends = ssem, rsem, 0, 0, []

    def sender(self, size):
        sem = self.ssem.at[self.n_send]
        self.n_send += 1
        self.ends.append((size, sem))
        return sem

    def receiver(self):
        sem = self.rsem.at[self.n_recv]
        self.n_recv += 1
        return sem

    def send(self, src, dst, device, ssem, rsem=None):
        rsem = self.receiver() if rsem is None else rsem
        pltpu.make_async_remote_copy(
            src_ref=src,
            dst_ref=dst,
            send_sem=ssem,
            recv_sem=rsem,
            device_id=device,
            device_id_type=pl.DeviceIdType.MESH,
        ).start()
        return dst, rsem

    def finish(self):
        for size, sem in self.ends:
            arrive((size, sem))


def arrive(flow):
    ref, sem = flow
    pltpu.make_async_copy(ref, ref, sem).wait()


def kernel(
    bits,
    pattern,
    frames_in,
    cot_in,
    taps,
    up_hbm,
    down_hbm,
    conv_out,
    gin_out,
    gup_out,
    gdown_out,
    cot,
    up_raw,
    down_raw,
    wu,
    wd,
    xs,
    gs,
    xt,
    pre,
    gh,
    hid,
    hidt,
    gpre,
    part,
    part_f,
    relay,
    got,
    term,
    rab,
    eab,
    side,
    ybig,
    comb,
    ysend,
    yrecv_down,
    yrecv_up,
    mine,
    halo,
    pad,
    mix,
    meet,
    wsem,
    ssem,
    rsem,
):
    rows, width = frames_in.shape
    frames = xs.at[0]
    yrecv = (yrecv_down, yrecv_up)
    chunk = rows // CHUNKS
    half = rows // 2
    ratio = wu.shape[1]
    s = lax.axis_index("seq")
    t = lax.axis_index("tensor")
    x, yh = s % 4, s // 4

    def flip(*which):
        out = t
        for b in which:
            out = out + (1 << b) * (1 - 2 * ((t // (1 << b)) % 2))
        return {"tensor": out}

    to_core, to_z1, to_z2, to_z6, to_y = flip(0), flip(1), flip(2), flip(2, 3), flip(4)
    x_right, x_left = {"seq": yh * 4 + (x + 1) % 4}, {"seq": yh * 4 + (x + 3) % 4}
    y_far = {"seq": (1 - yh) * 4 + x}
    s_next, s_prev = {"seq": (s + 1) % 8}, {"seq": (s + 7) % 8}
    net = Net(ssem, rsem)

    barrier = pltpu.get_barrier_semaphore()
    peers = (to_core, to_z1, to_z2, to_z6, to_y, x_right, x_left, y_far, s_next, s_prev)
    for peer in peers:
        pl.semaphore_signal(barrier, inc=1, device_id=peer, device_id_type=pl.DeviceIdType.MESH)

    def fetch(src, dst, i):
        copy = pltpu.make_async_copy(src, dst, wsem.at[i])
        copy.start()
        return copy

    copy_frames = fetch(frames_in, frames, 2)
    copy_up = fetch(up_hbm, up_raw, 0)
    copy_cot = fetch(cot_in, cot, 3)
    copy_down = fetch(down_hbm, down_raw, 1)
    pl.semaphore_wait(barrier, len(peers))

    def halo_send(ref, kind):
        out, into = net.sender(halo.at[kind]), net.receiver()
        net.send(ref.at[pl.ds(rows - 16, 16)], halo.at[kind, 0], s_next, out, into)
        net.send(ref.at[pl.ds(0, 16)], halo.at[kind, 1], s_prev, out, into)
        return halo.at[kind], into

    def ready(i, others):
        for other in others:
            pl.semaphore_signal(
                meet.at[i], inc=1, device_id=other, device_id_type=pl.DeviceIdType.MESH
            )

    def await_ready(i, others):
        pl.semaphore_wait(meet.at[i], len(others))

    def piece(c):
        return pl.ds(c * chunk, chunk)

    def small(c):
        return pl.ds(c * (rows // PIECES), rows // PIECES)

    def spread(own, dst):
        out = net.sender(dst.at[pl.ds(1, 5)])
        z2 = [net.send(own.at[small(c)], dst.at[3, small(c)], to_z2, out) for c in range(PIECES)]
        z1 = net.send(own, dst.at[2], to_z1, out)
        y = net.send(own, dst.at[5], to_y, out)
        core = net.send(own, dst.at[1], to_core, out)
        z4 = [(dst.at[4, pl.ds(h * half, half)], net.receiver()) for h in range(2)]
        return out, z2, z1, y, core, z4

    def forward(out, z2, z4, dst, part):
        each = PIECES // 4
        for c in range(part * each, (part + 1) * each):
            arrive(z2[c])
            net.send(dst.at[3, small(c)], dst.at[4, small(c)], to_z6, out, z4[2 * c // PIECES][1])

    cot_halo = halo_send(cot_in, 0)
    x_out, x_z2, x_z1, x_y, x_core, x_z4 = spread(frames_in, xs)

    level_of = []
    for b in range(5):
        found = jnp.int32(1)
        for lev in range(1, 5):
            found = jnp.where(bits[lev] == b, lev + 1, found)
        level_of.append(found)
    mask_of = [[jnp.float32(1.0)] * ratio] + [
        [
            sum(jnp.where(bits[lev] == b, pattern[k, lev], 0) for lev in range(5)).astype(F32)
            for k in range(ratio)
        ]
        for b in range(5)
    ]

    def build(raw, out):
        for k in range(ratio):
            out[0, k] = raw[0, k]
        for b in range(5):
            for k in range(ratio):
                out[b + 1, k] = (raw[level_of[b], k].astype(F32) * mask_of[b + 1][k]).astype(BF16)

    def accumulate(acc, lhs, weights, b, dot, first=False):
        def body(k, carry):
            value = dot(lhs[...], weights[b, k])
            if first:
                acc[k] = value
            else:
                acc[k] += value
            return carry

        lax.fori_loop(0, ratio, body, 0)

    def convolve(ref, kind, before, after):
        prev = halo[kind, 0].astype(F32)[15:16]
        nxt = halo[kind, 1].astype(F32)[0:1]
        pad[pl.ds(7, 1)] = jnp.where(s > 0, prev, 0.0)
        pad[pl.ds(8, rows)] = ref[...].astype(F32)
        pad[pl.ds(8 + rows, 1)] = jnp.where(s < 7, nxt, 0.0)
        return (
            before * pad[pl.ds(7, rows)] + taps[1:2] * pad[pl.ds(8, rows)] + after * pad[pl.ds(9, rows)]
        ).astype(BF16)

    copy_up.wait()
    build(up_raw, wu)
    copy_frames.wait()
    accumulate(pre, frames, wu, 0, dot_nn, first=True)
    forward(x_out, x_z2, x_z4, xs, 0)
    arrive(x_core)
    accumulate(pre, xs.at[1], wu, 1, dot_nn)
    forward(x_out, x_z2, x_z4, xs, 1)
    copy_down.wait()
    build(down_raw, wd)
    xt[0] = xs[0].T
    xt[1] = xs[1].T
    forward(x_out, x_z2, x_z4, xs, 2)
    arrive(x_y)
    accumulate(pre, xs.at[5], wu, 5, dot_nn)
    forward(x_out, x_z2, x_z4, xs, 3)
    copy_cot.wait()
    arrive(cot_halo)
    gs[0] = convolve(cot, 0, taps[2:3], taps[0:1])
    accumulate(pre, xs.at[3], wu, 3, dot_nn)
    arrive(x_z1)
    accumulate(pre, xs.at[2], wu, 2, dot_nn)
    for b in (5, 3, 2):
        xt[b] = xs[b].T
    for g in Y_FIRST:
        yrecv[g // 6][g % 6] = jnp.zeros(yrecv_up.shape[1:], BF16)

    def partial_rows(source, weights, b, dot, at):
        total = dot(source[0, at], weights[b, 0])
        for k in range(1, ratio):
            total += dot(source[k, at], weights[b, k])
        return total

    whole = pl.ds(0, rows)

    for h in range(2):
        arrive(x_z4[h])
        if h == 0:
            g_out, g_z2, g_z1, g_y, g_core, g_z4 = spread(gs.at[0], gs)
        at = pl.ds(h * half, half)

        def finish(k, carry, at=at):
            u = pre[k, at] + dot_nn(xs[4, at], wu[4, k])
            square = u * u
            inner = jnp.tanh(COEF * (u + 0.044715 * square * u))
            hid[k, at] = (0.5 * u * (1.0 + inner)).astype(BF16)
            pre[k, at] = 0.5 * (1.0 + inner) + 0.5 * u * (1.0 - inner * inner) * COEF * (
                1.0 + 3.0 * 0.044715 * square
            )
            return carry

        lax.fori_loop(0, ratio, finish, 0)
    for k in range(ratio):
        hidt[k] = hid[k].T

    phase_out = [net.sender(xs.at[pl.ds(1, 5)]) for _ in range(2)]
    phase_in = [(got.at[p, pl.ds(0, 4)], net.receiver()) for p in range(2)]

    def far_partial(phase, source, weights, dot):
        part[phase, 0] = partial_rows(source, weights, 4, dot, whole).astype(BF16)

    def far_send(phase):
        return [
            net.send(part.at[phase, 0, piece(c)], got.at[phase, 4, piece(c)], to_z6, phase_out[phase])
            for c in range(CHUNKS)
        ]

    def near_send(phase, slot, device):
        net.send(part.at[phase, slot], got.at[phase, slot], device, phase_out[phase], phase_in[phase][1])

    def near_partials(phase, source, weights, dot):
        for slot, b, device in ((2, 5, to_y), (3, 1, to_core), (1, 2, None)):
            part[phase, slot] = partial_rows(source, weights, b, dot, whole).astype(BF16)
            if device is not None:
                near_send(phase, slot, device)

    def kept_partials(phase, source, weights, dot):
        part_f[phase, 0] = partial_rows(source, weights, 3, dot, whole)
        part_f[phase, 1] = partial_rows(source, weights, 0, dot, whole)

    def combine(phase, z4):
        for c in range(CHUNKS):
            arrive(z4[c])
            at = piece(c)
            relay[phase, at] = (part_f[phase, 0, at] + got[phase, 4, at].astype(F32)).astype(BF16)
            net.send(
                relay.at[phase, at], got.at[phase, 0, at], to_z2, phase_out[phase], phase_in[phase][1]
            )

    def gather_sum(phase):
        arrive(phase_in[phase])
        total = part_f[phase, 1]
        for slot in range(4):
            total += got[phase, slot].astype(F32)
        return total.astype(BF16)

    scale = 1.0 / 64.0
    far, right, left = (x + 2) % 4, (x + 1) % 4, (x + 3) % 4
    group_out = {}
    flows = {}

    def halves(g):
        if g in Y_FIRST:
            i = Y_FIRST.index(g)
            first, second = pl.ds(0, ratio // 2), pl.ds(ratio // 2, ratio // 2)
            return comb, (lambda j: (i, j, first)), (lambda j: (i, j, second)), first
        return term, (lambda j: (g, j)), (lambda j: (g, 4 + j)), pl.ds(0, ratio)

    def send_across(g):
        group_out[g] = net.sender(term.at[g, pl.ds(0, 7)])
        i = Y_FIRST.index(g)
        flows[g] = net.send(term.at[g, pl.ds((1 - yh) * 4, 4)], ybig.at[i], y_far, group_out[g])

    def scatter_one(g):
        if g in Y_FIRST:
            i = Y_FIRST.index(g)
            arrive(flows[g])
            comb[i] = (term[g, pl.ds(yh * 4, 4)].astype(F32) + ybig[i].astype(F32)).astype(BF16)
        else:
            group_out[g] = net.sender(term.at[g, pl.ds(0, 7)])
        ref, a_at, b_at, ks = halves(g)
        out, via, end = group_out[g], net.receiver(), net.receiver()
        net.send(ref.at[a_at(far)], rab.at[g, 0, ks], x_right, out, via)
        net.send(ref.at[b_at(far)], rab.at[g, 1, ks], x_left, out, via)
        net.send(ref.at[b_at(right)], side.at[g, 0, 1, ks], x_right, out, end)
        net.send(ref.at[a_at(left)], side.at[g, 1, 0, ks], x_left, out, end)
        flows[g] = ((rab.at[g, :, ks], via), (side.at[g, :, :, ks], end))

    def scatter_two(g):
        ref, a_at, b_at, ks = halves(g)
        arrive(flows[g][0])
        end = flows[g][1][1]
        eab[g, 0, ks] = (rab[g, 0, ks].astype(F32) + ref[a_at(right)].astype(F32)).astype(BF16)
        net.send(eab.at[g, 0, ks], side.at[g, 0, 0, ks], x_right, group_out[g], end)
        eab[g, 1, ks] = (rab[g, 1, ks].astype(F32) + ref[b_at(left)].astype(F32)).astype(BF16)
        net.send(eab.at[g, 1, ks], side.at[g, 1, 1, ks], x_left, group_out[g], end)

    def side_sum(g, own, h, ks):
        return own.astype(F32) + side[g, 0, h, ks].astype(F32) + side[g, 1, h, ks].astype(F32)

    def scatter_three(g):
        arrive(flows[g][1])
        ref, a_at, b_at, ks = halves(g)
        if g in Y_FIRST:
            mine[g, ks] = side_sum(g, ref[a_at(x)], 0, ks)
            mine[g, pl.ds(ratio // 2, ratio // 2)] = side_sum(g, ref[b_at(x)], 1, ks)
            return
        ysend[g] = side_sum(g, term[g, (1 - yh) * 4 + x], 1 - yh, ks).astype(BF16)
        flows[g] = net.send(ysend.at[g], yrecv[g // 6].at[g % 6], y_far, group_out[g])
        mine[g] = side_sum(g, term[g, yh * 4 + x], yh, ks)

    def start(g):
        if g in Y_FIRST:
            send_across(g)
        else:
            scatter_one(g)

    def down_term(b):
        for k in range(ratio):
            value = dot_nn(hidt[k], gs[b]) * (mask_of[b][k] * scale)
            term[b, :, k] = value.astype(BF16).reshape(8, 32, width)
        start(b)

    def up_term(b):
        for k in range(ratio):
            value = dot_nn(xt[b], gpre[k]) * (mask_of[b][k] * scale)
            term[6 + b, :, k] = value.astype(BF16).reshape(8, 32, width)
        start(6 + b)

    down_term(0)
    arrive(g_core)
    down_term(1)
    accumulate(gh, gs.at[0], wd, 0, dot_nt, first=True)
    accumulate(gh, gs.at[1], wd, 1, dot_nt)
    far_partial(0, hid, wd, dot_nn)
    forward(g_out, g_z2, g_z4, gs, 0)
    arrive(g_y)
    down_term(5)
    accumulate(gh, gs.at[5], wd, 5, dot_nt)
    forward(g_out, g_z2, g_z4, gs, 1)
    scatter_two(0)
    kept_partials(0, hid, wd, dot_nn)
    forward(g_out, g_z2, g_z4, gs, 2)
    scatter_two(1)
    forward(g_out, g_z2, g_z4, gs, 3)
    down_term(3)
    near_partials(0, hid, wd, dot_nn)
    accumulate(gh, gs.at[3], wd, 3, dot_nt)
    arrive(g_z1)
    down_term(2)
    accumulate(gh, gs.at[2], wd, 2, dot_nt)
    scatter_two(5)
    xt[4] = xs[4].T
    for h in range(2):
        arrive(g_z4[h])
        if h == 0:
            ready(0, (to_core, to_z1))
            await_ready(0, (to_core, to_z1))
            mixed_z4 = far_send(0)
        else:
            near_send(0, 1, to_z1)
        at = pl.ds(h * half, half)

        def finish_grad(k, carry, at=at):
            gpre[k, at] = ((gh[k, at] + dot_nt(gs[4, at], wd[4, k])) * pre[k, at]).astype(BF16)
            return carry

        lax.fori_loop(0, ratio, finish_grad, 0)
        if h == 0:
            scatter_one(3)
    up_term(0)
    far_partial(1, gpre, wu, dot_nt)
    gin_z4 = far_send(1)
    down_term(4)
    scatter_two(2)
    up_term(1)
    up_term(2)
    up_term(5)
    scatter_two(3)
    up_term(4)
    up_term(3)
    near_partials(1, gpre, wu, dot_nt)
    kept_partials(1, gpre, wu, dot_nt)
    for g in (0, 1, 5):
        scatter_three(g)
    scatter_two(6)
    scatter_two(4)
    combine(0, mixed_z4)
    scatter_two(8)
    scatter_one(7)
    scatter_two(10)
    combine(1, gin_z4)
    near_send(1, 1, to_z1)
    for g in (2, 3):
        scatter_three(g)
    scatter_one(11)
    scatter_two(9)
    scatter_three(6)
    scatter_three(4)
    scatter_two(7)
    mix[...] = gather_sum(0)
    mix_halo = halo_send(mix, 1)
    scatter_two(11)
    scatter_three(8)
    scatter_three(10)
    scatter_three(9)

    def final(base, out):
        there = yrecv[base // 6]
        out[0] = mine[base] + there[0].astype(F32)
        for lev in range(5):
            b = 1 + bits[lev]
            out[lev + 1] = mine[base + b] + there[b].astype(F32)

    for g in (0, 1, 5, 2, 4):
        arrive(flows[g])
    final(0, gdown_out)
    arrive(mix_halo)
    conv_out[...] = convolve(mix, 1, taps[0:1], taps[2:3])
    scatter_three(7)
    scatter_three(11)
    gin_out[...] = gather_sum(1)
    for g in (6, 8, 10, 9):
        arrive(flows[g])
    final(6, gup_out)
    net.finish()


def write_kernel(*refs):
    ins, outs, sems = refs[:4], refs[4:8], refs[8]
    stores = [pltpu.make_async_copy(ins[i], outs[i], sems.at[i]) for i in range(4)]
    for store in stores:
        store.start()
    for store in stores:
        store.wait()


def local(frames, up_factors, down_factors, pattern, level_bits, taps, cotangent):
    rows, width = frames.shape
    factors, ratio, _, _ = up_factors.shape
    weights = (factors, ratio, width, width)
    tile = (ratio, 32, width)
    vmem = pl.BlockSpec(memory_space=pltpu.VMEM)
    smem = pl.BlockSpec(memory_space=pltpu.SMEM)
    anywhere = pl.BlockSpec(memory_space=pl.ANY)
    shape = jax.ShapeDtypeStruct
    results = (
        shape((rows, width), BF16),
        shape((rows, width), BF16),
        shape((factors,) + tile, F32),
        shape((factors,) + tile, F32),
    )
    held = tuple(pltpu.VMEM(each.shape, each.dtype) for each in results)
    computed = pl.pallas_call(
        kernel,
        out_shape=held,
        in_specs=[smem, smem, anywhere, anywhere, vmem, anywhere, anywhere],
        out_specs=(vmem,) * 4,
        scratch_shapes=[
            pltpu.VMEM((rows, width), BF16),
            pltpu.VMEM(weights, BF16),
            pltpu.VMEM(weights, BF16),
            pltpu.VMEM(weights, BF16),
            pltpu.VMEM(weights, BF16),
            pltpu.VMEM((6, rows, width), BF16),
            pltpu.VMEM((6, rows, width), BF16),
            pltpu.VMEM((6, width, rows), BF16),
            pltpu.VMEM((ratio, rows, width), F32),
            pltpu.VMEM((ratio, rows, width), F32),
            pltpu.VMEM((ratio, rows, width), BF16),
            pltpu.VMEM((ratio, width, rows), BF16),
            pltpu.VMEM((ratio, rows, width), BF16),
            pltpu.VMEM((2, 4, rows, width), BF16),
            pltpu.VMEM((2, 2, rows, width), F32),
            pltpu.VMEM((2, rows, width), BF16),
            pltpu.VMEM((2, 5, rows, width), BF16),
            pltpu.VMEM((12, 8) + tile, BF16),
            pltpu.VMEM((12, 2) + tile, BF16),
            pltpu.VMEM((12, 2) + tile, BF16),
            pltpu.VMEM((12, 2, 2) + tile, BF16),
            pltpu.VMEM((len(Y_FIRST), 4) + tile, BF16),
            pltpu.VMEM((len(Y_FIRST), 4) + tile, BF16),
            pltpu.VMEM((12,) + tile, BF16),
            pltpu.VMEM((6,) + tile, BF16),
            pltpu.VMEM((6,) + tile, BF16),
            pltpu.VMEM((12,) + tile, F32),
            pltpu.VMEM((2, 2, 16, width), BF16),
            pltpu.VMEM((rows + 16, width), F32),
            pltpu.VMEM((rows, width), BF16),
            pltpu.SemaphoreType.REGULAR((3,)),
            pltpu.SemaphoreType.DMA((8,)),
            pltpu.SemaphoreType.DMA((N_SENDS,)),
            pltpu.SemaphoreType.DMA((N_RECVS,)),
        ],
        compiler_params=pltpu.CompilerParams(
            collective_id=0, has_side_effects=True, vmem_limit_bytes=56 * 1024 * 1024
        ),
    )(level_bits, pattern, frames, cotangent, taps, up_factors, down_factors)
    return pl.pallas_call(
        write_kernel,
        out_shape=results,
        in_specs=[vmem] * 4,
        out_specs=(anywhere,) * 4,
        scratch_shapes=[pltpu.SemaphoreType.DMA((4,))],
        compiler_params=pltpu.CompilerParams(vmem_limit_bytes=4 * 1024 * 1024),
    )(*computed)


def solution(mesh):
    in_specs = (
        P("seq", "tensor"),
        P(None, "tensor", None, None),
        P(None, "tensor", None, None),
        P("tensor", None),
        P(),
        P(None, "tensor"),
        P("seq", "tensor"),
    )
    out_specs = (
        P("seq", "tensor"),
        P("seq", "tensor"),
        P(None, "tensor", "seq", None),
        P(None, "tensor", "seq", None),
    )
    return jax.shard_map(local, mesh=mesh, in_specs=in_specs, out_specs=out_specs, check_vma=False)
```

```python
import functools

import jax
import jax.numpy as jnp
from jax import lax
from jax.experimental import pallas as pl
from jax.experimental.pallas import tpu as pltpu
from jax.sharding import PartitionSpec as P

COEF = 0.7978845608028654
F32 = jnp.float32
BF16 = jnp.bfloat16
CHUNKS = 4
PIECES = 16
N_SENDS = 18
N_RECVS = 90
Y_FIRST = (3, 7, 11)


def dot_nn(a, b):
    return jnp.dot(a, b, preferred_element_type=F32)


def dot_nt(a, b):
    return lax.dot_general(a, b, (((1,), (1,)), ((), ())), preferred_element_type=F32)


class Net:
    def __init__(self, ssem, rsem):
        self.ssem, self.rsem, self.n_send, self.n_recv, self.ends = ssem, rsem, 0, 0, []

    def sender(self, size):
        sem = self.ssem.at[self.n_send]
        self.n_send += 1
        self.ends.append((size, sem))
        return sem

    def receiver(self):
        sem = self.rsem.at[self.n_recv]
        self.n_recv += 1
        return sem

    def send(self, src, dst, device, ssem, rsem=None):
        rsem = self.receiver() if rsem is None else rsem
        pltpu.make_async_remote_copy(
            src_ref=src,
            dst_ref=dst,
            send_sem=ssem,
            recv_sem=rsem,
            device_id=device,
            device_id_type=pl.DeviceIdType.MESH,
        ).start()
        return dst, rsem

    def finish(self):
        for size, sem in self.ends:
            arrive((size, sem))


def arrive(flow):
    ref, sem = flow
    pltpu.make_async_copy(ref, ref, sem).wait()


def kernel(
    bits,
    pattern,
    frames_in,
    cot_in,
    taps,
    up_hbm,
    down_hbm,
    conv_out,
    gin_out,
    gup_out,
    gdown_out,
    cot,
    up_raw,
    down_raw,
    wu,
    wd,
    xs,
    gs,
    xt,
    pre,
    gh,
    hid,
    hidt,
    gpre,
    part,
    part_f,
    relay,
    got,
    term,
    rab,
    eab,
    side,
    ybig,
    comb,
    ysend,
    yrecv_down,
    yrecv_up,
    mine,
    halo,
    pad,
    mix,
    meet,
    wsem,
    ssem,
    rsem,
):
    rows, width = frames_in.shape
    frames = xs.at[0]
    yrecv = (yrecv_down, yrecv_up)
    chunk = rows // CHUNKS
    half = rows // 2
    ratio = wu.shape[1]
    s = lax.axis_index("seq")
    t = lax.axis_index("tensor")
    x, yh = s % 4, s // 4

    def flip(*which):
        out = t
        for b in which:
            out = out + (1 << b) * (1 - 2 * ((t // (1 << b)) % 2))
        return {"tensor": out}

    to_core, to_z1, to_z2, to_z6, to_y = flip(0), flip(1), flip(2), flip(2, 3), flip(4)
    x_right, x_left = {"seq": yh * 4 + (x + 1) % 4}, {"seq": yh * 4 + (x + 3) % 4}
    y_far = {"seq": (1 - yh) * 4 + x}
    s_next, s_prev = {"seq": (s + 1) % 8}, {"seq": (s + 7) % 8}
    net = Net(ssem, rsem)

    barrier = pltpu.get_barrier_semaphore()
    peers = (to_core, to_z1, to_z2, to_z6, to_y, x_right, x_left, y_far, s_next, s_prev)
    for peer in peers:
        pl.semaphore_signal(barrier, inc=1, device_id=peer, device_id_type=pl.DeviceIdType.MESH)

    def fetch(src, dst, i):
        copy = pltpu.make_async_copy(src, dst, wsem.at[i])
        copy.start()
        return copy

    copy_frames = fetch(frames_in, frames, 2)
    copy_up = fetch(up_hbm, up_raw, 0)
    copy_cot = fetch(cot_in, cot, 3)
    copy_down = fetch(down_hbm, down_raw, 1)
    pl.semaphore_wait(barrier, len(peers))

    def halo_send(ref, kind):
        out, into = net.sender(halo.at[kind]), net.receiver()
        net.send(ref.at[pl.ds(rows - 16, 16)], halo.at[kind, 0], s_next, out, into)
        net.send(ref.at[pl.ds(0, 16)], halo.at[kind, 1], s_prev, out, into)
        return halo.at[kind], into

    def ready(i, others):
        for other in others:
            pl.semaphore_signal(
                meet.at[i], inc=1, device_id=other, device_id_type=pl.DeviceIdType.MESH
            )

    def await_ready(i, others):
        pl.semaphore_wait(meet.at[i], len(others))

    def piece(c):
        return pl.ds(c * chunk, chunk)

    def small(c):
        return pl.ds(c * (rows // PIECES), rows // PIECES)

    def spread(own, dst):
        out = net.sender(dst.at[pl.ds(1, 5)])
        z2 = [net.send(own.at[small(c)], dst.at[3, small(c)], to_z2, out) for c in range(PIECES)]
        z1 = net.send(own, dst.at[2], to_z1, out)
        y = net.send(own, dst.at[5], to_y, out)
        core = net.send(own, dst.at[1], to_core, out)
        z4 = [(dst.at[4, pl.ds(h * half, half)], net.receiver()) for h in range(2)]
        return out, z2, z1, y, core, z4

    def forward(out, z2, z4, dst, part):
        each = PIECES // 4
        for c in range(part * each, (part + 1) * each):
            arrive(z2[c])
            net.send(dst.at[3, small(c)], dst.at[4, small(c)], to_z6, out, z4[2 * c // PIECES][1])

    cot_halo = halo_send(cot_in, 0)
    x_out, x_z2, x_z1, x_y, x_core, x_z4 = spread(frames_in, xs)

    level_of = []
    for b in range(5):
        found = jnp.int32(1)
        for lev in range(1, 5):
            found = jnp.where(bits[lev] == b, lev + 1, found)
        level_of.append(found)
    mask_of = [[jnp.float32(1.0)] * ratio] + [
        [
            sum(jnp.where(bits[lev] == b, pattern[k, lev], 0) for lev in range(5)).astype(F32)
            for k in range(ratio)
        ]
        for b in range(5)
    ]

    def build(raw, out):
        for k in range(ratio):
            out[0, k] = raw[0, k]
        for b in range(5):
            for k in range(ratio):
                out[b + 1, k] = (raw[level_of[b], k].astype(F32) * mask_of[b + 1][k]).astype(BF16)

    def accumulate(acc, lhs, weights, b, dot, first=False):
        def body(k, carry):
            value = dot(lhs[...], weights[b, k])
            if first:
                acc[k] = value
            else:
                acc[k] += value
            return carry

        lax.fori_loop(0, ratio, body, 0)

    def convolve(ref, kind, before, after):
        prev = halo[kind, 0].astype(F32)[15:16]
        nxt = halo[kind, 1].astype(F32)[0:1]
        pad[pl.ds(7, 1)] = jnp.where(s > 0, prev, 0.0)
        pad[pl.ds(8, rows)] = ref[...].astype(F32)
        pad[pl.ds(8 + rows, 1)] = jnp.where(s < 7, nxt, 0.0)
        return (
            before * pad[pl.ds(7, rows)] + taps[1:2] * pad[pl.ds(8, rows)] + after * pad[pl.ds(9, rows)]
        ).astype(BF16)

    copy_up.wait()
    build(up_raw, wu)
    copy_frames.wait()
    accumulate(pre, frames, wu, 0, dot_nn, first=True)
    forward(x_out, x_z2, x_z4, xs, 0)
    arrive(x_core)
    accumulate(pre, xs.at[1], wu, 1, dot_nn)
    forward(x_out, x_z2, x_z4, xs, 1)
    copy_down.wait()
    build(down_raw, wd)
    xt[0] = xs[0].T
    xt[1] = xs[1].T
    forward(x_out, x_z2, x_z4, xs, 2)
    arrive(x_y)
    accumulate(pre, xs.at[5], wu, 5, dot_nn)
    forward(x_out, x_z2, x_z4, xs, 3)
    copy_cot.wait()
    arrive(cot_halo)
    gs[0] = convolve(cot, 0, taps[2:3], taps[0:1])
    accumulate(pre, xs.at[3], wu, 3, dot_nn)
    arrive(x_z1)
    accumulate(pre, xs.at[2], wu, 2, dot_nn)
    for b in (5, 3, 2):
        xt[b] = xs[b].T
    for g in Y_FIRST:
        yrecv[g // 6][g % 6] = jnp.zeros(yrecv_up.shape[1:], BF16)

    def partial_rows(source, weights, b, dot, at):
        total = dot(source[0, at], weights[b, 0])
        for k in range(1, ratio):
            total += dot(source[k, at], weights[b, k])
        return total

    whole = pl.ds(0, rows)

    g_out, g_z2, g_z1, g_y, g_core, g_z4 = spread(gs.at[0], gs)
    for h in range(2):
        arrive(x_z4[h])
        at = pl.ds(h * half, half)

        def finish(k, carry, at=at):
            u = pre[k, at] + dot_nn(xs[4, at], wu[4, k])
            square = u * u
            inner = jnp.tanh(COEF * (u + 0.044715 * square * u))
            hid[k, at] = (0.5 * u * (1.0 + inner)).astype(BF16)
            pre[k, at] = 0.5 * (1.0 + inner) + 0.5 * u * (1.0 - inner * inner) * COEF * (
                1.0 + 3.0 * 0.044715 * square
            )
            return carry

        lax.fori_loop(0, ratio, finish, 0)
    for k in range(ratio):
        hidt[k] = hid[k].T

    phase_out = [net.sender(xs.at[pl.ds(1, 5)]) for _ in range(2)]
    phase_in = [(got.at[p, pl.ds(0, 4)], net.receiver()) for p in range(2)]

    def far_partial(phase, source, weights, dot):
        part[phase, 0] = partial_rows(source, weights, 4, dot, whole).astype(BF16)

    def far_send(phase):
        return [
            net.send(part.at[phase, 0, piece(c)], got.at[phase, 4, piece(c)], to_z6, phase_out[phase])
            for c in range(CHUNKS)
        ]

    def near_send(phase, slot, device):
        net.send(part.at[phase, slot], got.at[phase, slot], device, phase_out[phase], phase_in[phase][1])

    def near_partials(phase, source, weights, dot):
        for slot, b, device in ((2, 5, to_y), (3, 1, to_core), (1, 2, None)):
            part[phase, slot] = partial_rows(source, weights, b, dot, whole).astype(BF16)
            if device is not None:
                near_send(phase, slot, device)

    def kept_partials(phase, source, weights, dot):
        part_f[phase, 0] = partial_rows(source, weights, 3, dot, whole)
        part_f[phase, 1] = partial_rows(source, weights, 0, dot, whole)

    def combine(phase, z4):
        for c in range(CHUNKS):
            arrive(z4[c])
            at = piece(c)
            relay[phase, at] = (part_f[phase, 0, at] + got[phase, 4, at].astype(F32)).astype(BF16)
            net.send(
                relay.at[phase, at], got.at[phase, 0, at], to_z2, phase_out[phase], phase_in[phase][1]
            )

    def gather_sum(phase):
        arrive(phase_in[phase])
        total = part_f[phase, 1]
        for slot in range(4):
            total += got[phase, slot].astype(F32)
        return total.astype(BF16)

    scale = 1.0 / 64.0
    far, right, left = (x + 2) % 4, (x + 1) % 4, (x + 3) % 4
    group_out = {}
    flows = {}

    def halves(g):
        if g in Y_FIRST:
            i = Y_FIRST.index(g)
            first, second = pl.ds(0, ratio // 2), pl.ds(ratio // 2, ratio // 2)
            return comb, (lambda j: (i, j, first)), (lambda j: (i, j, second)), first
        return term, (lambda j: (g, j)), (lambda j: (g, 4 + j)), pl.ds(0, ratio)

    def send_across(g):
        group_out[g] = net.sender(term.at[g, pl.ds(0, 7)])
        i = Y_FIRST.index(g)
        flows[g] = net.send(term.at[g, pl.ds((1 - yh) * 4, 4)], ybig.at[i], y_far, group_out[g])

    def scatter_one(g):
        if g in Y_FIRST:
            i = Y_FIRST.index(g)
            arrive(flows[g])
            comb[i] = (term[g, pl.ds(yh * 4, 4)].astype(F32) + ybig[i].astype(F32)).astype(BF16)
        else:
            group_out[g] = net.sender(term.at[g, pl.ds(0, 7)])
        ref, a_at, b_at, ks = halves(g)
        out, via, end = group_out[g], net.receiver(), net.receiver()
        net.send(ref.at[a_at(far)], rab.at[g, 0, ks], x_right, out, via)
        net.send(ref.at[b_at(far)], rab.at[g, 1, ks], x_left, out, via)
        net.send(ref.at[b_at(right)], side.at[g, 0, 1, ks], x_right, out, end)
        net.send(ref.at[a_at(left)], side.at[g, 1, 0, ks], x_left, out, end)
        flows[g] = ((rab.at[g, :, ks], via), (side.at[g, :, :, ks], end))

    def scatter_two(g):
        ref, a_at, b_at, ks = halves(g)
        arrive(flows[g][0])
        end = flows[g][1][1]
        eab[g, 0, ks] = (rab[g, 0, ks].astype(F32) + ref[a_at(right)].astype(F32)).astype(BF16)
        net.send(eab.at[g, 0, ks], side.at[g, 0, 0, ks], x_right, group_out[g], end)
        eab[g, 1, ks] = (rab[g, 1, ks].astype(F32) + ref[b_at(left)].astype(F32)).astype(BF16)
        net.send(eab.at[g, 1, ks], side.at[g, 1, 1, ks], x_left, group_out[g], end)

    def side_sum(g, own, h, ks):
        return own.astype(F32) + side[g, 0, h, ks].astype(F32) + side[g, 1, h, ks].astype(F32)

    def scatter_three(g):
        arrive(flows[g][1])
        ref, a_at, b_at, ks = halves(g)
        if g in Y_FIRST:
            mine[g, ks] = side_sum(g, ref[a_at(x)], 0, ks)
            mine[g, pl.ds(ratio // 2, ratio // 2)] = side_sum(g, ref[b_at(x)], 1, ks)
            return
        ysend[g] = side_sum(g, term[g, (1 - yh) * 4 + x], 1 - yh, ks).astype(BF16)
        flows[g] = net.send(ysend.at[g], yrecv[g // 6].at[g % 6], y_far, group_out[g])
        mine[g] = side_sum(g, term[g, yh * 4 + x], yh, ks)

    def start(g):
        if g in Y_FIRST:
            send_across(g)
        else:
            scatter_one(g)

    def down_term(b):
        for k in range(ratio):
            value = dot_nn(hidt[k], gs[b]) * (mask_of[b][k] * scale)
            term[b, :, k] = value.astype(BF16).reshape(8, 32, width)
        start(b)

    def up_term(b):
        for k in range(ratio):
            value = dot_nn(xt[b], gpre[k]) * (mask_of[b][k] * scale)
            term[6 + b, :, k] = value.astype(BF16).reshape(8, 32, width)
        start(6 + b)

    down_term(0)
    arrive(g_core)
    down_term(1)
    accumulate(gh, gs.at[0], wd, 0, dot_nt, first=True)
    accumulate(gh, gs.at[1], wd, 1, dot_nt)
    far_partial(0, hid, wd, dot_nn)
    forward(g_out, g_z2, g_z4, gs, 0)
    arrive(g_y)
    down_term(5)
    accumulate(gh, gs.at[5], wd, 5, dot_nt)
    forward(g_out, g_z2, g_z4, gs, 1)
    scatter_two(0)
    kept_partials(0, hid, wd, dot_nn)
    forward(g_out, g_z2, g_z4, gs, 2)
    scatter_two(1)
    forward(g_out, g_z2, g_z4, gs, 3)
    down_term(3)
    near_partials(0, hid, wd, dot_nn)
    accumulate(gh, gs.at[3], wd, 3, dot_nt)
    arrive(g_z1)
    down_term(2)
    accumulate(gh, gs.at[2], wd, 2, dot_nt)
    scatter_two(5)
    xt[4] = xs[4].T
    for h in range(2):
        arrive(g_z4[h])
        if h == 0:
            ready(0, (to_core, to_z1))
            await_ready(0, (to_core, to_z1))
            mixed_z4 = far_send(0)
        else:
            near_send(0, 1, to_z1)
        at = pl.ds(h * half, half)

        def finish_grad(k, carry, at=at):
            gpre[k, at] = ((gh[k, at] + dot_nt(gs[4, at], wd[4, k])) * pre[k, at]).astype(BF16)
            return carry

        lax.fori_loop(0, ratio, finish_grad, 0)
        if h == 0:
            scatter_one(3)
    up_term(0)
    far_partial(1, gpre, wu, dot_nt)
    gin_z4 = far_send(1)
    down_term(4)
    scatter_two(2)
    up_term(1)
    up_term(2)
    up_term(5)
    scatter_two(3)
    up_term(4)
    up_term(3)
    near_partials(1, gpre, wu, dot_nt)
    kept_partials(1, gpre, wu, dot_nt)
    for g in (0, 1, 5):
        scatter_three(g)
    scatter_two(6)
    scatter_two(4)
    combine(0, mixed_z4)
    scatter_two(8)
    scatter_one(7)
    scatter_two(10)
    combine(1, gin_z4)
    near_send(1, 1, to_z1)
    for g in (2, 3):
        scatter_three(g)
    scatter_one(11)
    scatter_two(9)
    scatter_three(6)
    scatter_three(4)
    scatter_two(7)
    mix[...] = gather_sum(0)
    mix_halo = halo_send(mix, 1)
    scatter_two(11)
    scatter_three(8)
    scatter_three(10)
    scatter_three(9)

    def final(base, out):
        there = yrecv[base // 6]
        out[0] = mine[base] + there[0].astype(F32)
        for lev in range(5):
            b = 1 + bits[lev]
            out[lev + 1] = mine[base + b] + there[b].astype(F32)

    for g in (0, 1, 5, 2, 4):
        arrive(flows[g])
    final(0, gdown_out)
    arrive(mix_halo)
    conv_out[...] = convolve(mix, 1, taps[0:1], taps[2:3])
    scatter_three(7)
    scatter_three(11)
    gin_out[...] = gather_sum(1)
    for g in (6, 8, 10, 9):
        arrive(flows[g])
    final(6, gup_out)
    net.finish()


def write_kernel(*refs):
    ins, outs, sems = refs[:4], refs[4:8], refs[8]
    stores = [pltpu.make_async_copy(ins[i], outs[i], sems.at[i]) for i in range(4)]
    for store in stores:
        store.start()
    for store in stores:
        store.wait()


def local(frames, up_factors, down_factors, pattern, level_bits, taps, cotangent):
    rows, width = frames.shape
    factors, ratio, _, _ = up_factors.shape
    weights = (factors, ratio, width, width)
    tile = (ratio, 32, width)
    vmem = pl.BlockSpec(memory_space=pltpu.VMEM)
    smem = pl.BlockSpec(memory_space=pltpu.SMEM)
    anywhere = pl.BlockSpec(memory_space=pl.ANY)
    shape = jax.ShapeDtypeStruct
    results = (
        shape((rows, width), BF16),
        shape((rows, width), BF16),
        shape((factors,) + tile, F32),
        shape((factors,) + tile, F32),
    )
    held = tuple(pltpu.VMEM(each.shape, each.dtype) for each in results)
    computed = pl.pallas_call(
        kernel,
        out_shape=held,
        in_specs=[smem, smem, anywhere, anywhere, vmem, anywhere, anywhere],
        out_specs=(vmem,) * 4,
        scratch_shapes=[
            pltpu.VMEM((rows, width), BF16),
            pltpu.VMEM(weights, BF16),
            pltpu.VMEM(weights, BF16),
            pltpu.VMEM(weights, BF16),
            pltpu.VMEM(weights, BF16),
            pltpu.VMEM((6, rows, width), BF16),
            pltpu.VMEM((6, rows, width), BF16),
            pltpu.VMEM((6, width, rows), BF16),
            pltpu.VMEM((ratio, rows, width), F32),
            pltpu.VMEM((ratio, rows, width), F32),
            pltpu.VMEM((ratio, rows, width), BF16),
            pltpu.VMEM((ratio, width, rows), BF16),
            pltpu.VMEM((ratio, rows, width), BF16),
            pltpu.VMEM((2, 4, rows, width), BF16),
            pltpu.VMEM((2, 2, rows, width), F32),
            pltpu.VMEM((2, rows, width), BF16),
            pltpu.VMEM((2, 5, rows, width), BF16),
            pltpu.VMEM((12, 8) + tile, BF16),
            pltpu.VMEM((12, 2) + tile, BF16),
            pltpu.VMEM((12, 2) + tile, BF16),
            pltpu.VMEM((12, 2, 2) + tile, BF16),
            pltpu.VMEM((len(Y_FIRST), 4) + tile, BF16),
            pltpu.VMEM((len(Y_FIRST), 4) + tile, BF16),
            pltpu.VMEM((12,) + tile, BF16),
            pltpu.VMEM((6,) + tile, BF16),
            pltpu.VMEM((6,) + tile, BF16),
            pltpu.VMEM((12,) + tile, F32),
            pltpu.VMEM((2, 2, 16, width), BF16),
            pltpu.VMEM((rows + 16, width), F32),
            pltpu.VMEM((rows, width), BF16),
            pltpu.SemaphoreType.REGULAR((3,)),
            pltpu.SemaphoreType.DMA((8,)),
            pltpu.SemaphoreType.DMA((N_SENDS,)),
            pltpu.SemaphoreType.DMA((N_RECVS,)),
        ],
        compiler_params=pltpu.CompilerParams(
            collective_id=0, has_side_effects=True, vmem_limit_bytes=56 * 1024 * 1024
        ),
    )(level_bits, pattern, frames, cotangent, taps, up_factors, down_factors)
    return pl.pallas_call(
        write_kernel,
        out_shape=results,
        in_specs=[vmem] * 4,
        out_specs=(anywhere,) * 4,
        scratch_shapes=[pltpu.SemaphoreType.DMA((4,))],
        compiler_params=pltpu.CompilerParams(vmem_limit_bytes=4 * 1024 * 1024),
    )(*computed)


def solution(mesh):
    in_specs = (
        P("seq", "tensor"),
        P(None, "tensor", None, None),
        P(None, "tensor", None, None),
        P("tensor", None),
        P(),
        P(None, "tensor"),
        P("seq", "tensor"),
    )
    out_specs = (
        P("seq", "tensor"),
        P("seq", "tensor"),
        P(None, "tensor", "seq", None),
        P(None, "tensor", "seq", None),
    )
    return jax.shard_map(local, mesh=mesh, in_specs=in_specs, out_specs=out_specs, check_vma=False)
```
